512 devices in a mesh: ctx: 64 (over y, z), head: 8 (over x, core).
Axes of the slice: x: 4, y: 4, z: 16, core: 2. Of those that a mesh axis runs over, the one named last changes fastest.
Arguments:
- lin_query: bfloat16 [8192, 64, 128], P('ctx', 'head'), may hold values from -6 to 6
- lin_key: bfloat16 [8192, 64, 128], P('ctx', 'head'), may hold values from -6 to 6
- lin_value: bfloat16 [8192, 64, 128], P('ctx', 'head'), may hold values from -18 to 18
- log_decay: float32 [64, 8192], P('head', 'ctx'), may hold values from -1 to 0
- norm_gain: float32 [64, 128], P('head'), may hold values from 0.5 to 1.5
- attn_query: bfloat16 [8192, 64, 128], P('ctx', 'head'), may hold values from -30 to 30
- attn_key: bfloat16 [8192, 8, 128], P('ctx', 'head'), may hold values from -16 to 16
- attn_value: bfloat16 [8192, 8, 128], P('ctx', 'head'), may hold values from -6 to 6
Outputs:
- lin_out: bfloat16 [8192, 64, 128], P('ctx', 'head')
- attn_out: bfloat16 [8192, 64, 128], P('ctx', 'head')
The draws below stay inside these ranges and needn't reach their ends.
All inputs are finite; a program needn't handle non-finite values.
Results may differ from the reference program's by a relative error of at most 0.0055.
Values may be sent and summed in bfloat16 or wider, within the bound.
No kernel may reach another device: no remote copies, remote signals or barrier semaphores. Data moves between devices by JAX's collectives and lax.ppermute only.
A program may use at most 192 MiB of HBM per device.

```python
import math
import jax
import jax.numpy as jnp
from jax import lax

QUERY_HEADS = 64
HD = 128
KV = 8
TOK_DEV = 128
SEQUENCE_LENGTH = 8192


def draw_lin_value(key, part):
    head_rank = jnp.arange(QUERY_HEADS, dtype=jnp.float32) / max(QUERY_HEADS - 1, 1)
    noise_base = jnp.clip(jax.random.normal(key, (SEQUENCE_LENGTH, QUERY_HEADS, HD), jnp.float32), -6.0, 6.0)
    head_scale = jnp.exp(math.log(3.0) * head_rank)
    return (noise_base * head_scale[None, :, None]).astype(jnp.bfloat16)


def draw_log_decay(key, part):
    key_sequence = jax.random.split(key, 6)
    slow_share = 0.5
    slow_heads = jax.random.uniform(key_sequence[0], (QUERY_HEADS,), jnp.float32) < slow_share
    fast_rate = jnp.exp(jax.random.uniform(key_sequence[1], (QUERY_HEADS,), jnp.float32, math.log(1.0 / 50.0), math.log(1.0 / 30.0)))
    slow_rate = jnp.exp(jax.random.uniform(key_sequence[2], (QUERY_HEADS,), jnp.float32, math.log(0.1), math.log(0.6))) / SEQUENCE_LENGTH
    per_head_decay = jnp.where(slow_heads, slow_rate, fast_rate)
    block_factor = jnp.exp(jax.random.uniform(key_sequence[3], (QUERY_HEADS, SEQUENCE_LENGTH // TOK_DEV), jnp.float32, math.log(0.7), math.log(1.4)))
    position_weight = jnp.repeat(block_factor, TOK_DEV, axis=1)
    spike_location = jax.random.randint(key_sequence[4], (QUERY_HEADS, 2), 0, SEQUENCE_LENGTH)
    token_position = jnp.arange(SEQUENCE_LENGTH)
    spike_found = jnp.any(token_position[None, None, :] == spike_location[:, :, None], axis=1)
    spike_penalty = jnp.log(jax.random.uniform(key_sequence[5], (QUERY_HEADS, SEQUENCE_LENGTH), jnp.float32, 0.5, 0.8))
    return (-per_head_decay[:, None] * position_weight + jnp.where(spike_found, spike_penalty, 0.0)).astype(jnp.float32)


def attention_pair(key):
    query_shape = (SEQUENCE_LENGTH, QUERY_HEADS, HD)
    key_shape = (SEQUENCE_LENGTH, KV, HD)
    query_base = jnp.clip(jax.random.normal(jax.random.fold_in(key, 13), query_shape, jnp.float32), -6.0, 6.0)
    key_base = 2.5 * jnp.clip(jax.random.normal(jax.random.fold_in(key, 11), key_shape, jnp.float32), -6.0, 6.0)
    return (query_base, key_base)


def draw_attn_query(key, part):
    return attention_pair(key)[0].astype(jnp.bfloat16)


def draw_attn_key(key, part):
    return attention_pair(key)[1].astype(jnp.bfloat16)


def shard_levels(key, shape, pieces, low, top_value):
    gain = 1.0
    for position, blocks in pieces:
        draws = jax.random.uniform(jax.random.fold_in(jax.random.fold_in(key, 6), position), (blocks,), jnp.float32, low / len(pieces), top_value / len(pieces))
        gain = gain * jnp.repeat(jnp.exp(draws), shape[position] // blocks).reshape((-1,) + (1,) * (len(shape) - 1 - position))
    return gain


def gaussian(rng, dims, deviation, bound, cuts=(), kind=jnp.bfloat16):
    loudness = shard_levels(rng, dims, cuts, -0.22, 0.18) if cuts else 1.0
    drawn = jax.random.normal(rng, dims, jnp.float32) * deviation * loudness
    return jnp.minimum(jnp.maximum(drawn, -bound), bound).astype(kind)


def setup_inputs(seed: int = 0) -> dict:
    arg_keys = jax.random.split(jax.random.key(seed), 9)
    lin_query = gaussian(arg_keys[0], (SEQUENCE_LENGTH, QUERY_HEADS, HD), 1.0, 6.0, ((0, 64), (1, 8)))
    lin_key = gaussian(arg_keys[1], (SEQUENCE_LENGTH, QUERY_HEADS, HD), 1.0, 6.0, ((0, 64), (1, 8)))
    lin_value = draw_lin_value(jax.random.fold_in(arg_keys[8], 71), 0)
    log_decay = draw_log_decay(jax.random.fold_in(arg_keys[8], 71), 0)
    norm_gain = jnp.clip(1.0 + 0.1 * jax.random.normal(arg_keys[4], (QUERY_HEADS, HD), jnp.float32), 0.5, 1.5)
    attn_query = draw_attn_query(jax.random.fold_in(arg_keys[8], 71), 0)
    attn_key = draw_attn_key(jax.random.fold_in(arg_keys[8], 71), 0)
    attn_value = gaussian(arg_keys[7], (SEQUENCE_LENGTH, KV, HD), 1.0, 6.0, ((0, 64), (1, 8)))
    return {"lin_query": lin_query, "lin_key": lin_key, "lin_value": lin_value, "log_decay": log_decay, "norm_gain": norm_gain, "attn_query": attn_query, "attn_key": attn_key, "attn_value": attn_value}


def round_half(values):
    return lax.optimization_barrier(values.astype(jnp.bfloat16)).astype(jnp.float32)

def act_round(values):
    return round_half(jax.nn.silu(values.astype(jnp.float32)))

def lightning_block(state_now, block_in):
    query_blk, key_blk, value_blk, decay_blk = block_in
    act_query = act_round(query_blk)
    act_key = act_round(key_blk)
    act_value = act_round(value_blk)
    cumulative = jnp.cumsum(decay_blk, axis=1)
    token_position = jnp.arange(query_blk.shape[0])
    causal = token_position[:, None] >= token_position[None, :]
    spread = cumulative[:, :, None] - cumulative[:, None, :]
    decay_matrix = jnp.exp(jnp.where(causal[None], spread, -1e+30))
    scores = jnp.einsum('thd,shd->hts', act_query, act_key, precision=lax.Precision.HIGHEST)
    weights = round_half(scores * decay_matrix)
    inner_part = jnp.einsum('hts,shd->thd', weights, act_value, precision=lax.Precision.HIGHEST)
    last_sum = cumulative[:, -1]
    key_factor = jnp.exp(last_sum[None, :] - cumulative.T)
    scaled_keys = round_half(act_key * key_factor[:, :, None])
    local_state = jnp.einsum('shd,she->hde', scaled_keys, act_value, precision=lax.Precision.HIGHEST)
    outer_part = jnp.einsum('thd,hde->the', act_query, state_now, precision=lax.Precision.HIGHEST)
    mixed_out = inner_part + outer_part * jnp.exp(cumulative.T)[:, :, None]
    state_next = jnp.exp(last_sum)[:, None, None] * state_now + local_state
    return (state_next, mixed_out)

def lightning_layer(lin_query, lin_key, lin_value, log_decay, norm_gain):
    blocks = SEQUENCE_LENGTH // TOK_DEV
    shaped = (blocks, TOK_DEV, QUERY_HEADS, HD)
    decay_blocks = log_decay.reshape(QUERY_HEADS, blocks, TOK_DEV).transpose(1, 0, 2)
    start_state = jnp.zeros((QUERY_HEADS, HD, HD), jnp.float32)
    final_state, mixed_out = lax.scan(lightning_block, start_state, (lin_query.reshape(shaped), lin_key.reshape(shaped), lin_value.reshape(shaped), decay_blocks))
    mixed_out = mixed_out.reshape(SEQUENCE_LENGTH, QUERY_HEADS, HD)
    mean_square = lax.optimization_barrier(jnp.sum(mixed_out * mixed_out, axis=(1, 2))) / (QUERY_HEADS * HD)
    inverse = lax.rsqrt(mean_square + 1e-06)
    return (mixed_out * inverse[:, None, None] * norm_gain[None]).astype(jnp.bfloat16)

def softmax_layer(attn_query, attn_key, attn_value):
    group = QUERY_HEADS // KV
    block_rows = 64
    keys_full = attn_key.astype(jnp.float32)
    values_full = attn_value.astype(jnp.float32)
    key_pos = jnp.arange(SEQUENCE_LENGTH)

    def one_block(block_start):
        query_blk = lax.dynamic_slice_in_dim(attn_query, block_start, block_rows, 0)
        query_blk = query_blk.astype(jnp.float32).reshape(block_rows, KV, group, HD)
        scores = jnp.einsum('bgrd,sgd->bgrs', query_blk, keys_full, precision=lax.Precision.HIGHEST) * HD ** (-0.5)
        query_pos = block_start + jnp.arange(block_rows)
        visible = query_pos[:, None] >= key_pos[None, :]
        masked = jnp.where(visible[:, None, None, :], scores, -1e+30)
        running_max = lax.optimization_barrier(jnp.max(masked, axis=3))
        prob_rows = jnp.where(visible[:, None, None, :], jnp.exp(scores - running_max[..., None]), 0.0)
        totals = lax.optimization_barrier(jnp.sum(prob_rows, axis=3))
        prob_rounded = round_half(prob_rows)
        summed = jnp.einsum('bgrs,sgd->bgrd', prob_rounded, values_full, precision=lax.Precision.HIGHEST)
        return (summed / totals[..., None]).reshape(block_rows, QUERY_HEADS, HD)
    starts = (jnp.arange(SEQUENCE_LENGTH // block_rows) * block_rows).astype(jnp.int32)
    outputs = lax.map(one_block, starts)
    return outputs.reshape(SEQUENCE_LENGTH, QUERY_HEADS, HD).astype(jnp.bfloat16)

def reference(lin_query, lin_key, lin_value, log_decay, norm_gain, attn_query, attn_key, attn_value):
    lin_out = lightning_layer(lin_query, lin_key, lin_value, log_decay, norm_gain)
    attn_out = softmax_layer(attn_query, attn_key, attn_value)
    return (lin_out, attn_out)
```

```python
import jax
import jax.numpy as jnp
from jax import lax
from jax.experimental import pallas as pl
from jax.experimental.pallas import tpu as pltpu
from jax.sharding import PartitionSpec as P

QUERY_HEADS = 64
HD = 128
TOK = 128
HEADS = 8
ROWS = TOK * HEADS
Y, Z = 4, 16
SLICE = ROWS // Z
STATE_ROWS = SLICE + 16
STAT_ROWS = 32
LOG2E = 1.4426950408889634
SCALE2 = LOG2E * HD ** (-0.5)
NEG = -1e30
F32, BF16 = jnp.float32, jnp.bfloat16
Z_GROUPS = [[y * Z + z for z in range(Z)] for y in range(Y)]
Y_GROUPS = [[y * Z + z for y in range(Y)] for z in range(Z)]


def split3(x):
    high = x.astype(BF16)
    rest = x - high.astype(F32)
    mid = rest.astype(BF16)
    low = (rest - mid.astype(F32)).astype(BF16)
    return high, mid, low


def scalar_rows(x):
    high, mid, low = (part.astype(F32) for part in split3(x))
    row = lax.broadcasted_iota(jnp.int32, (16, 128), 0)
    out = jnp.where(row == 0, high, jnp.where(row == 1, mid, jnp.where(row == 2, low, 0.0)))
    return out.astype(BF16)


def scalar_back(rows):
    rows = rows.astype(F32)
    return rows[0:1] + rows[1:2] + rows[2:3]


def silu(ref):
    x = ref[...].astype(F32)
    return x / (1.0 + jnp.exp(-x))


def local_kernel(q_ref, k_ref, v_ref, decay_ref, pay_ref, inner_ref, act_ref, ecum_ref, sq, sk, sv):
    sq[...] = silu(q_ref)
    sk[...] = silu(k_ref)
    sv[...] = silu(v_ref)
    lane = lax.broadcasted_iota(jnp.int32, (HEADS, TOK), 1)
    cum = decay_ref[...]
    step = 1
    while step < TOK:
        cum = cum + jnp.where(lane >= step, pltpu.roll(cum, step, 1), 0.0)
        step *= 2
    cum_col = jnp.transpose(jnp.concatenate([cum] * (TOK // HEADS), axis=0))
    ecum_ref[...] = jnp.exp(cum_col)
    causal = lax.broadcasted_iota(jnp.int32, (TOK, TOK), 0) >= lax.broadcasted_iota(
        jnp.int32, (TOK, TOK), 1
    )
    for h in range(HEADS):
        mine = pl.ds(h, TOK, stride=HEADS)
        aq = sq[mine, :].astype(BF16)
        ak = sk[mine, :].astype(BF16)
        av = sv[mine, :].astype(BF16)
        act_ref[h] = aq
        row = cum[h : h + 1, :]
        col = cum_col[:, h : h + 1]
        last = row[:, TOK - 1 : TOK]
        scores = lax.dot_general(aq, ak, (((1,), (1,)), ((), ())), preferred_element_type=F32)
        weights = (scores * jnp.exp(jnp.where(causal, col - row, NEG))).astype(BF16)
        inner_ref[h] = jnp.dot(weights, av, preferred_element_type=F32)
        scaled = (ak.astype(F32) * jnp.exp(last - col)).astype(BF16)
        state = lax.dot_general(scaled, av, (((0,), (0,)), ((), ())), preferred_element_type=F32)
        extra = scalar_rows(jnp.broadcast_to(last, (1, 128)))
        for half in range(2):
            pay_ref[2 * h + half, 0:SLICE, :] = state[half * SLICE : (half + 1) * SLICE].astype(BF16)
            pay_ref[2 * h + half, SLICE:STATE_ROWS, :] = extra


def row_kernel(got_ref, q_ref, before_ref, lead_ref, pay_ref):
    run = jnp.zeros((SLICE, 128), F32)
    total = jnp.zeros((1, 128), F32)
    for z in range(Z):
        before_ref[z] = run
        lead_ref[z : z + 1, :] = total
        decay = scalar_back(got_ref[z, SLICE:STATE_ROWS, :])
        run = run * jnp.exp(decay) + got_ref[z, 0:SLICE, :].astype(F32)
        total = total + decay
    extra = scalar_rows(total)
    for y in range(Y):
        pay_ref[y, 0:SLICE, :] = run.astype(BF16)
        pay_ref[y, SLICE:STATE_ROWS, :] = extra
        pay_ref[y, STATE_ROWS:, :] = q_ref[...]


def carry_kernel(pos_ref, got_ref, before_ref, lead_ref, out_ref):
    mine = pos_ref[0]
    carry = jnp.zeros((SLICE, 128), F32)
    for y in range(Y - 1):
        decay = scalar_back(got_ref[y, SLICE:STATE_ROWS, :])
        new = carry * jnp.exp(decay) + got_ref[y, 0:SLICE, :].astype(F32)
        carry = jnp.where(y < mine, new, carry)
    for z in range(Z):
        out_ref[z] = (before_ref[z] + jnp.exp(lead_ref[z : z + 1, :]) * carry).astype(BF16)


def mix_kernel(act_ref, inner_ref, ecum_ref, prior_ref, mixed_ref, square_ref):
    squares = jnp.zeros((TOK, HD), F32)
    for h in range(HEADS):
        outer = jnp.dot(act_ref[h], prior_ref[h * HD : (h + 1) * HD, :], preferred_element_type=F32)
        mixed = inner_ref[h] + outer * ecum_ref[:, h : h + 1]
        squares = squares + mixed * mixed
        mixed_ref[pl.ds(h, TOK, stride=HEADS), :] = mixed
    square_ref[...] = jnp.sum(jnp.transpose(squares), axis=0, keepdims=True)


QT = 256
KEYS = Z * TOK


def attend_kernel(pos_ref, got_ref, kv_ref, out_ref, keys, vaug, stats):
    my_y, my_z = pos_ref[0], pos_ref[1]
    for z in range(Z):
        keys[z * TOK : (z + 1) * TOK, :] = kv_ref[z, 0:TOK, :]
        vaug[z * TOK : (z + 1) * TOK, 0:HD] = kv_ref[z, TOK : 2 * TOK, :]
    vaug[:, HD:] = jnp.ones((KEYS, HD), BF16)

    def tile(y, i, masked):
        start = pl.multiple_of(i * QT, QT)
        q = got_ref[y, pl.ds(STATE_ROWS + start, QT), :]
        s = lax.dot_general(q, keys[...], (((1,), (1,)), ((), ())), preferred_element_type=F32)
        if masked:
            row = lax.broadcasted_iota(jnp.int32, (QT, KEYS), 0)
            key = lax.broadcasted_iota(jnp.int32, (QT, KEYS), 1)
            pos = my_z * TOK + (row + start) // HEADS
            s = jnp.where(pos >= key, s, NEG)
        top = jnp.max(s, axis=1, keepdims=True) * SCALE2
        p = jnp.exp2(s * SCALE2 - top).astype(BF16)
        acc = jnp.dot(p, vaug[...], preferred_element_type=F32)
        total = acc[:, HD:]
        out_ref[y, pl.ds(STAT_ROWS + start, QT), :] = (acc[:, :HD] / total).astype(BF16)
        lse = top + jnp.log(total) * LOG2E
        for b in range(QT // 128):
            stats[pl.ds(i * (QT // 128) + b, 1), :] = jnp.transpose(lse[b * 128 : (b + 1) * 128])[0:1]

    for y in range(Y):

        @pl.when(my_y < y)
        def _():
            lax.fori_loop(0, ROWS // QT, lambda i, c: (tile(y, i, False), c)[1], 0)

        @pl.when(my_y == y)
        def _():
            lax.fori_loop(0, ROWS // QT, lambda i, c: (tile(y, i, True), c)[1], 0)

        @pl.when(my_y > y)
        def _():
            stats[...] = jnp.full((HEADS, 128), NEG, F32)
            out_ref[y, STAT_ROWS:, :] = jnp.zeros((ROWS, HD), BF16)

        high, mid, low = split3(stats[...])
        zero = jnp.zeros((HEADS, 128), BF16)
        out_ref[y, 0:16, :] = jnp.concatenate([high, mid], axis=0)
        out_ref[y, 16:32, :] = jnp.concatenate([low, zero], axis=0)


def merge_kernel(got_ref, out_ref):
    lse = []
    for y in range(Y):
        first = got_ref[y, 0:16, :].astype(F32)
        second = got_ref[y, 16:32, :].astype(F32)
        lse.append(first[0:8] + first[8:16] + second[0:8])
    top = jnp.maximum(jnp.maximum(lse[0], lse[1]), jnp.maximum(lse[2], lse[3]))
    w = [jnp.exp2(x - top) for x in lse]
    total = w[0] + w[1] + w[2] + w[3]
    w = [x / total for x in w]
    for b in range(ROWS // 128):
        rows = slice(STAT_ROWS + b * 128, STAT_ROWS + (b + 1) * 128)
        acc = jnp.zeros((128, HD), F32)
        for y in range(Y):
            col = jnp.transpose(jnp.broadcast_to(w[y][b : b + 1, :], (128, 128)))
            acc = acc + col * got_ref[y, rows, :].astype(F32)
        out_ref[b * 128 : (b + 1) * 128, :] = acc.astype(BF16)


def shape(*dims, kind=BF16):
    return jax.ShapeDtypeStruct(dims, kind)


VM = pl.BlockSpec(memory_space=pltpu.VMEM)
SM = pl.BlockSpec(memory_space=pltpu.SMEM)


def params(mib=16):
    return pltpu.CompilerParams(vmem_limit_bytes=mib << 20)


def cost(flops, nbytes, exps=0):
    return pl.CostEstimate(flops=flops, bytes_accessed=nbytes, transcendentals=exps)


def local(lin_query, lin_key, lin_value, log_decay, norm_gain, attn_query, attn_key, attn_value):
    index = lax.axis_index("ctx")
    pos = jnp.stack([index // Z, index % Z]).astype(jnp.int32)

    kv = jnp.concatenate([attn_key.reshape(TOK, HD), attn_value.reshape(TOK, HD)], axis=0)
    kv_row = lax.all_gather(kv, "ctx", axis_index_groups=Z_GROUPS)

    flat = lambda x: x.reshape(ROWS, HD)
    pay, inner, act, ecum = pl.pallas_call(
        local_kernel,
        out_shape=(
            shape(Z, STATE_ROWS, 128),
            shape(HEADS, TOK, HD, kind=F32),
            shape(HEADS, TOK, HD),
            shape(TOK, 128, kind=F32),
        ),
        in_specs=[VM] * 4,
        out_specs=(VM,) * 4,
        scratch_shapes=[pltpu.VMEM((ROWS, HD), F32)] * 3,
        compiler_params=params(),
        cost_estimate=cost(4 * 2 * 8 * 128**3, 2 << 20, 1 << 19),
        name="local_part",
    )(flat(lin_query), flat(lin_key), flat(lin_value), log_decay)
    got = lax.all_to_all(pay, "ctx", 0, 0, axis_index_groups=Z_GROUPS)

    before, lead, pay = pl.pallas_call(
        row_kernel,
        out_shape=(
            shape(Z, SLICE, 128, kind=F32),
            shape(Z, 128, kind=F32),
            shape(Y, STATE_ROWS + ROWS, 128),
        ),
        in_specs=[VM] * 2,
        out_specs=(VM,) * 3,
        compiler_params=params(),
        cost_estimate=cost(1 << 19, 3 << 20),
        name="row_scan",
    )(got, flat(attn_query))
    got = lax.all_to_all(pay, "ctx", 0, 0, axis_index_groups=Y_GROUPS)

    pay = pl.pallas_call(
        carry_kernel,
        out_shape=shape(Z, SLICE, 128),
        grid=(1,),
        in_specs=[
            SM,
            pl.BlockSpec((Y, STATE_ROWS, 128), lambda i: (0, 0, 0)),
            pl.BlockSpec((Z, SLICE, 128), lambda i: (0, 0, 0)),
            pl.BlockSpec((Z, 128), lambda i: (0, 0)),
        ],
        out_specs=pl.BlockSpec((Z, SLICE, 128), lambda i: (0, 0, 0)),
        compiler_params=params(),
        cost_estimate=cost(1 << 19, 1 << 20),
        name="carry_in",
    )(pos, got, before, lead)
    prior = lax.all_to_all(pay, "ctx", 0, 0, axis_index_groups=Z_GROUPS)

    mixed, squares = pl.pallas_call(
        mix_kernel,
        out_shape=(shape(ROWS, HD, kind=F32), shape(1, TOK, kind=F32)),
        in_specs=[VM] * 4,
        out_specs=(VM,) * 2,
        compiler_params=params(),
        cost_estimate=cost(2 * 8 * 128**3, 2 << 20),
        name="mix",
    )(act, inner, ecum, prior.reshape(ROWS, HD))
    total = lax.psum(squares, "head")
    inverse = lax.rsqrt(total[0] / (QUERY_HEADS * HD) + 1e-06)
    lin_out = mixed.reshape(TOK, HEADS, HD) * inverse[:, None, None] * norm_gain[None]
    lin_out = lin_out.astype(BF16)

    got, squares = lax.optimization_barrier((got, squares))
    pay = pl.pallas_call(
        attend_kernel,
        out_shape=shape(Y, STAT_ROWS + ROWS, HD),
        in_specs=[SM, VM, VM],
        out_specs=VM,
        scratch_shapes=[
            pltpu.VMEM((KEYS, HD), BF16),
            pltpu.VMEM((KEYS, 2 * HD), BF16),
            pltpu.VMEM((HEADS, 128), F32),
        ],
        compiler_params=params(40),
        cost_estimate=cost(3 * 2 * 4 * ROWS * KEYS * HD, 4 << 20, 4 * ROWS * KEYS),
        name="attend",
    )(pos, got, kv_row)
    got = lax.all_to_all(pay, "ctx", 0, 0, axis_index_groups=Y_GROUPS)
    attn_out = pl.pallas_call(
        merge_kernel,
        out_shape=shape(ROWS, HD),
        in_specs=[VM],
        out_specs=VM,
        compiler_params=params(),
        cost_estimate=cost(1 << 20, 2 << 20),
        name="merge",
    )(got)
    return lin_out, attn_out.reshape(TOK, HEADS, HD)


def solution(mesh):
    act = P("ctx", "head", None)
    return jax.shard_map(
        local,
        mesh=mesh,
        in_specs=(act, act, act, P("head", "ctx"), P("head", None), act, act, act),
        out_specs=(act, act),
        check_vma=False,
    )
```

```python
import jax
import jax.numpy as jnp
from jax import lax
from jax.experimental import pallas as pl
from jax.experimental.pallas import tpu as pltpu
from jax.sharding import PartitionSpec as P

QUERY_HEADS = 64
HD = 128
TOK = 128
HEADS = 8
ROWS = TOK * HEADS
Y, Z = 4, 16
SLICE = ROWS // Z
STATE_ROWS = SLICE + 16
STAT_ROWS = 32
SPARE = 96
KV_ROWS = 2 * TOK + SPARE
LOG2E = 1.4426950408889634
SCALE2 = LOG2E * HD ** (-0.5)
NEG = -1e30
F32, BF16 = jnp.float32, jnp.bfloat16
Z_GROUPS = [[y * Z + z for z in range(Z)] for y in range(Y)]
PAIR_GROUPS = [[y * Z + 2 * p, y * Z + 2 * p + 1] for y in range(Y) for p in range(Z // 2)]
SPREAD_GROUPS = [[y * Z + 2 * p + odd for p in range(Z // 2)] for y in range(Y) for odd in range(2)]
Y_GROUPS = [[y * Z + z for y in range(Y)] for z in range(Z)]


def split3(x):
    high = x.astype(BF16)
    rest = x - high.astype(F32)
    mid = rest.astype(BF16)
    low = (rest - mid.astype(F32)).astype(BF16)
    return high, mid, low


def scalar_rows(x):
    high, mid, low = (part.astype(F32) for part in split3(x))
    row = lax.broadcasted_iota(jnp.int32, (16, 128), 0)
    out = jnp.where(row == 0, high, jnp.where(row == 1, mid, jnp.where(row == 2, low, 0.0)))
    return out.astype(BF16)


def scalar_back(rows):
    rows = rows.astype(F32)
    return rows[0:1] + rows[1:2] + rows[2:3]


def silu(ref):
    x = ref[...].astype(F32)
    return x / (1.0 + jnp.exp(-x))


def local_kernel(
    q_hbm, k_hbm, v_hbm, decay_hbm, pay_ref, inner_ref, act_ref, ecum_ref,
    q_ref, k_ref, v_ref, decay_ref, sq, sk, sv, sems,
):
    pairs = ((decay_hbm, decay_ref), (k_hbm, k_ref), (v_hbm, v_ref), (q_hbm, q_ref))
    copies = [pltpu.make_async_copy(a, b, sems.at[i]) for i, (a, b) in enumerate(pairs)]
    for copy in copies:
        copy.start()
    copies[0].wait()
    lane = lax.broadcasted_iota(jnp.int32, (HEADS, TOK), 1)
    cum = decay_ref[...]
    step = 1
    while step < TOK:
        cum = cum + jnp.where(lane >= step, pltpu.roll(cum, step, 1), 0.0)
        step *= 2
    cum_col = jnp.transpose(jnp.concatenate([cum] * (TOK // HEADS), axis=0))
    ecum_ref[...] = jnp.exp(cum_col)
    causal = lax.broadcasted_iota(jnp.int32, (TOK, TOK), 0) >= lax.broadcasted_iota(
        jnp.int32, (TOK, TOK), 1
    )
    copies[1].wait()
    sk[...] = silu(k_ref)
    copies[2].wait()
    sv[...] = silu(v_ref)
    copies[3].wait()
    sq[...] = silu(q_ref)
    for h in range(HEADS):
        mine = pl.ds(h, TOK, stride=HEADS)
        aq = sq[mine, :].astype(BF16)
        ak = sk[mine, :].astype(BF16)
        av = sv[mine, :].astype(BF16)
        act_ref[h] = aq
        row = cum[h : h + 1, :]
        col = cum_col[:, h : h + 1]
        last = row[:, TOK - 1 : TOK]
        scores = lax.dot_general(aq, ak, (((1,), (1,)), ((), ())), preferred_element_type=F32)
        weights = (scores * jnp.exp(jnp.where(causal, col - row, NEG))).astype(BF16)
        inner_ref[h] = jnp.dot(weights, av, preferred_element_type=F32)
        scaled = (ak.astype(F32) * jnp.exp(last - col)).astype(BF16)
        state = lax.dot_general(scaled, av, (((0,), (0,)), ((), ())), preferred_element_type=F32)
        extra = scalar_rows(jnp.broadcast_to(last, (1, 128)))
        for half in range(2):
            pay_ref[2 * h + half, 0:SLICE, :] = state[half * SLICE : (half + 1) * SLICE].astype(BF16)
            pay_ref[2 * h + half, SLICE:STATE_ROWS, :] = extra


def keep_kernel(pay_in, inner_ref, act_ref, ecum_ref, pay_out):
    pass


def row_kernel(got_ref, q_ref, pay_ref):
    run = jnp.zeros((SLICE, 128), F32)
    total = jnp.zeros((1, 128), F32)
    for z in range(Z):
        decay = scalar_back(got_ref[z, SLICE:STATE_ROWS, :])
        run = run * jnp.exp(decay) + got_ref[z, 0:SLICE, :].astype(F32)
        total = total + decay
    extra = scalar_rows(total)
    for y in range(Y):
        pay_ref[y, 0:SLICE, :] = run.astype(BF16)
        pay_ref[y, SLICE:STATE_ROWS, :] = extra
        pay_ref[y, STATE_ROWS:, :] = q_ref[...]


def carry_kernel(pos_ref, rows_ref, got_ref, out_ref):
    mine = pos_ref[0]
    run = jnp.zeros((SLICE, 128), F32)
    for y in range(Y - 1):
        decay = scalar_back(rows_ref[y, SLICE:STATE_ROWS, :])
        new = run * jnp.exp(decay) + rows_ref[y, 0:SLICE, :].astype(F32)
        run = jnp.where(y < mine, new, run)
    for z in range(Z):
        out_ref[z] = run.astype(BF16)
        decay = scalar_back(got_ref[z, SLICE:STATE_ROWS, :])
        run = run * jnp.exp(decay) + got_ref[z, 0:SLICE, :].astype(F32)


def mix_kernel(act_ref, inner_ref, ecum_ref, prior_ref, mixed_ref, square_ref):
    squares = jnp.zeros((TOK, HD), F32)
    for h in range(HEADS):
        outer = jnp.dot(act_ref[h], prior_ref[h * HD : (h + 1) * HD, :], preferred_element_type=F32)
        mixed = inner_ref[h] + outer * ecum_ref[:, h : h + 1]
        squares = squares + mixed * mixed
        mixed_ref[pl.ds(h, TOK, stride=HEADS), :] = mixed
    square_ref[...] = jnp.broadcast_to(jnp.sum(jnp.transpose(squares), axis=0, keepdims=True), (8, TOK))


QT = 512
CHUNK = 256
KEYS = Z * TOK


def attend_kernel(pos_ref, q_ref, kv_hbm, out_ref, keys, vaug, s_even, s_odd, stats, sems):
    my_y, my_z = pos_ref[0], pos_ref[1]
    get_keys = pltpu.make_async_copy(kv_hbm.at[:, 0:TOK, :], keys, sems.at[0])
    get_values = pltpu.make_async_copy(kv_hbm.at[:, TOK : 2 * TOK, :], vaug.at[:, :, 0:HD], sems.at[1])
    get_keys.start()
    get_values.start()
    vaug[:, :, HD:] = jnp.ones((Z, TOK, HD), BF16)
    get_keys.wait()
    get_values.wait()
    held = (s_even, s_odd)
    tiles, chunks, blocks = ROWS // QT, KEYS // CHUNK, CHUNK // TOK

    def score(y, i, j, top, masked):
        q = q_ref[y, STATE_ROWS + i * QT : STATE_ROWS + (i + 1) * QT, :]
        part = keys[j * blocks : (j + 1) * blocks].reshape(CHUNK, HD)
        s = lax.dot_general(q, part, (((1,), (1,)), ((), ())), preferred_element_type=F32)
        if masked:
            row = lax.broadcasted_iota(jnp.int32, (QT, CHUNK), 0)
            key = lax.broadcasted_iota(jnp.int32, (QT, CHUNK), 1)
            pos = my_z * TOK - j * CHUNK + (row + i * QT) // HEADS
            s = jnp.where(pos >= key, s, NEG)
        held[i % 2][:, j * CHUNK : (j + 1) * CHUNK] = s
        for lanes in range(blocks):
            new = s[:, lanes * 128 : (lanes + 1) * 128]
            top = new if top is None else jnp.maximum(top, new)
        return top

    def unit(y, masked):
        top = None
        for j in range(chunks):
            top = score(y, 0, j, top, masked)
        for i in range(tiles):
            shift = jnp.max(top, axis=1, keepdims=True) * SCALE2
            top = acc = None
            for j in range(chunks):
                if i + 1 < tiles:
                    top = score(y, i + 1, j, top, masked)
                s = held[i % 2][:, j * CHUNK : (j + 1) * CHUNK]
                p = jnp.exp2(s * SCALE2 - shift).astype(BF16)
                part = vaug[j * blocks : (j + 1) * blocks].reshape(CHUNK, 2 * HD)
                new = jnp.dot(p, part, preferred_element_type=F32)
                acc = new if acc is None else acc + new
            total = acc[:, HD:]
            out_ref[y, STAT_ROWS + i * QT : STAT_ROWS + (i + 1) * QT, :] = (acc[:, :HD] / total).astype(BF16)
            lse = shift + jnp.log(total) * LOG2E
            for b in range(QT // 128):
                at = i * (QT // 128) + b
                stats[at : at + 1, :] = jnp.transpose(lse[b * 128 : (b + 1) * 128])[0:1]
        high, mid, low = split3(stats[...])
        zero = jnp.zeros((HEADS, 128), BF16)
        out_ref[y, 0:16, :] = jnp.concatenate([high, mid], axis=0)
        out_ref[y, 16:32, :] = jnp.concatenate([low, zero], axis=0)

    def skip(y, carry):
        out_ref[y, 0:16, :] = jnp.concatenate([jnp.full((8, 128), NEG, BF16), jnp.zeros((8, 128), BF16)], axis=0)
        out_ref[y, 16:, :] = jnp.zeros((ROWS + 16, HD), BF16)
        return carry

    def other(y, carry):
        unit(y, False)
        return carry

    lax.fori_loop(0, my_y, skip, 0)
    unit(my_y, True)
    lax.fori_loop(my_y + 1, Y, other, 0)


def merge_kernel(got_ref, out_ref):
    lse = []
    for y in range(Y):
        first = got_ref[y, 0:16, :].astype(F32)
        second = got_ref[y, 16:32, :].astype(F32)
        lse.append(first[0:8] + first[8:16] + second[0:8])
    top = jnp.maximum(jnp.maximum(lse[0], lse[1]), jnp.maximum(lse[2], lse[3]))
    w = [jnp.exp2(x - top) for x in lse]
    total = w[0] + w[1] + w[2] + w[3]
    w = [x / total for x in w]
    for b in range(ROWS // 128):
        rows = slice(STAT_ROWS + b * 128, STAT_ROWS + (b + 1) * 128)
        acc = jnp.zeros((128, HD), F32)
        for y in range(Y):
            col = jnp.transpose(jnp.broadcast_to(w[y][b : b + 1, :], (128, 128)))
            acc = acc + col * got_ref[y, rows, :].astype(F32)
        out_ref[b * 128 : (b + 1) * 128, :] = acc.astype(BF16)


def shape(*dims, kind=BF16):
    return jax.ShapeDtypeStruct(dims, kind)


VM = pl.BlockSpec(memory_space=pltpu.VMEM)
SM = pl.BlockSpec(memory_space=pltpu.SMEM)
HB = pl.BlockSpec(memory_space=pltpu.HBM)
ANY = pl.BlockSpec(memory_space=pl.ANY)


def params(mib=16):
    return pltpu.CompilerParams(vmem_limit_bytes=mib << 20)


def cost(flops, nbytes, exps=0):
    return pl.CostEstimate(flops=flops, bytes_accessed=nbytes, transcendentals=exps)


def local(lin_query, lin_key, lin_value, log_decay, norm_gain, attn_query, attn_key, attn_value):
    index = lax.axis_index("ctx")
    pos = jnp.stack([lax.shift_right_logical(index, 4), index & (Z - 1)]).astype(jnp.int32)

    flat = lambda x: x.reshape(ROWS, HD)
    kv = [attn_key.reshape(TOK, HD), attn_value.reshape(TOK, HD), jnp.zeros((SPARE, HD), BF16)]
    kv = jnp.concatenate(kv, axis=0)
    kv = lax.all_gather(kv, "ctx", axis_index_groups=PAIR_GROUPS)
    kv, pos, lin_query, lin_key, lin_value = lax.optimization_barrier(
        (kv, pos, lin_query, lin_key, lin_value)
    )
    kv_row = lax.all_gather(kv, "ctx", axis_index_groups=SPREAD_GROUPS).reshape(Z, KV_ROWS, HD)
    pay, inner, act, ecum = pl.pallas_call(
        local_kernel,
        out_shape=(
            shape(Z, STATE_ROWS, 128),
            shape(HEADS, TOK, HD, kind=F32),
            shape(HEADS, TOK, HD),
            shape(TOK, 128, kind=F32),
        ),
        in_specs=[ANY] * 4,
        out_specs=(VM,) * 4,
        scratch_shapes=[pltpu.VMEM((ROWS, HD), BF16)] * 3
        + [pltpu.VMEM((HEADS, TOK), F32)]
        + [pltpu.VMEM((ROWS, HD), F32)] * 3
        + [pltpu.SemaphoreType.DMA((4,))],
        compiler_params=params(62),
        cost_estimate=cost(1, 1),
        name="local_part",
    )(flat(lin_query), flat(lin_key), flat(lin_value), log_decay)
    pay = pl.pallas_call(
        keep_kernel,
        out_shape=shape(Z, STATE_ROWS, 128),
        in_specs=[ANY] * 4,
        out_specs=ANY,
        input_output_aliases={0: 0},
        compiler_params=params(62),
        cost_estimate=cost(1, 1),
        name="keep",
    )(pay, inner, act, ecum)
    got = lax.all_to_all(pay, "ctx", 0, 0, axis_index_groups=Z_GROUPS)
    got, query = lax.optimization_barrier((got, flat(attn_query)))

    pay = pl.pallas_call(
        row_kernel,
        out_shape=shape(Y, STATE_ROWS + ROWS, 128),
        in_specs=[VM, VM],
        out_specs=VM,
        compiler_params=params(),
        cost_estimate=cost(1, 1),
        name="row_scan",
    )(got, query)
    queries = lax.all_to_all(pay, "ctx", 0, 0, axis_index_groups=Y_GROUPS)

    pay = pl.pallas_call(
        carry_kernel,
        out_shape=shape(Z, SLICE, 128),
        grid=(1,),
        in_specs=[
            SM,
            pl.BlockSpec((Y, STATE_ROWS, 128), lambda i: (0, 0, 0)),
            pl.BlockSpec((Z, STATE_ROWS, 128), lambda i: (0, 0, 0)),
        ],
        out_specs=pl.BlockSpec((Z, SLICE, 128), lambda i: (0, 0, 0)),
        compiler_params=params(),
        cost_estimate=cost(1, 1),
        name="carry_in",
    )(pos, queries, got)
    pay, queries = lax.optimization_barrier((pay, queries))
    prior = lax.all_to_all(pay, "ctx", 0, 0, axis_index_groups=Z_GROUPS)

    pay = pl.pallas_call(
        attend_kernel,
        out_shape=shape(Y, STAT_ROWS + ROWS, HD),
        in_specs=[SM, VM, HB],
        out_specs=VM,
        scratch_shapes=[
            pltpu.VMEM((Z, TOK, HD), BF16),
            pltpu.VMEM((Z, TOK, 2 * HD), BF16),
            pltpu.VMEM((QT, KEYS), F32),
            pltpu.VMEM((QT, KEYS), F32),
            pltpu.VMEM((HEADS, 128), F32),
            pltpu.SemaphoreType.DMA((2,)),
        ],
        compiler_params=params(62),
        cost_estimate=cost(3 * 2 * 4 * ROWS * KEYS * HD, 4 << 20, 4 * ROWS * KEYS),
        name="attend",
    )(pos, queries, kv_row)
    pay, prior = lax.optimization_barrier((pay, prior))
    got = lax.all_to_all(pay, "ctx", 0, 0, axis_index_groups=Y_GROUPS)

    mixed, squares = pl.pallas_call(
        mix_kernel,
        out_shape=(shape(ROWS, HD, kind=F32), shape(8, TOK, kind=F32)),
        in_specs=[VM] * 4,
        out_specs=(VM,) * 2,
        compiler_params=params(),
        cost_estimate=cost(2 * 8 * 128**3, 2 << 20),
        name="mix",
    )(act, inner, ecum, prior.reshape(ROWS, HD))

    total = jnp.sum(lax.all_gather(squares, "head")[:, 0], axis=0)
    inverse = lax.rsqrt(total / (QUERY_HEADS * HD) + 1e-06)
    lin_out = mixed.reshape(TOK, HEADS, HD) * inverse[:, None, None] * norm_gain[None]
    lin_out = lin_out.astype(BF16)

    attn_out = pl.pallas_call(
        merge_kernel,
        out_shape=shape(ROWS, HD),
        in_specs=[VM],
        out_specs=VM,
        compiler_params=params(),
        cost_estimate=cost(1 << 20, 2 << 20),
        name="merge",
    )(got)
    return lin_out, attn_out.reshape(TOK, HEADS, HD)


def solution(mesh):
    act = P("ctx", "head", None)
    return jax.shard_map(
        local,
        mesh=mesh,
        in_specs=(act, act, act, P("head", "ctx"), P("head", None), act, act, act),
        out_specs=(act, act),
        check_vma=False,
    )
```

```python
import jax
import jax.numpy as jnp
from jax import lax
from jax.experimental import pallas as pl
from jax.experimental.pallas import tpu as pltpu
from jax.sharding import PartitionSpec as P

QUERY_HEADS = 64
HD = 128
TOK = 128
HEADS = 8
ROWS = TOK * HEADS
Y, Z = 4, 16
SLICE = ROWS // Z
STATE_ROWS = SLICE + 16
STAT_ROWS = 32
SPARE = 88
KV_ROWS = 2 * TOK + SPARE
LOG2E = 1.4426950408889634
SCALE2 = LOG2E * HD ** (-0.5)
NEG = -1e30
F32, BF16 = jnp.float32, jnp.bfloat16
Z_GROUPS = [[y * Z + z for z in range(Z)] for y in range(Y)]
PAIR_GROUPS = [[y * Z + 2 * p, y * Z + 2 * p + 1] for y in range(Y) for p in range(Z // 2)]
SPREAD_GROUPS = [[y * Z + 2 * p + odd for p in range(Z // 2)] for y in range(Y) for odd in range(2)]
Y_GROUPS = [[y * Z + z for y in range(Y)] for z in range(Z)]


def split3(x):
    high = x.astype(BF16)
    rest = x - high.astype(F32)
    mid = rest.astype(BF16)
    low = (rest - mid.astype(F32)).astype(BF16)
    return high, mid, low


def scalar_rows(x):
    high, mid, low = (part.astype(F32) for part in split3(x))
    row = lax.broadcasted_iota(jnp.int32, (16, 128), 0)
    out = jnp.where(row == 0, high, jnp.where(row == 1, mid, jnp.where(row == 2, low, 0.0)))
    return out.astype(BF16)


def scalar_back(rows):
    rows = rows.astype(F32)
    return rows[0:1] + rows[1:2] + rows[2:3]


def silu(ref):
    x = ref[...].astype(F32)
    return x / (1.0 + jnp.exp(-x))


def local_kernel(
    q_hbm, k_hbm, v_hbm, decay_hbm, pay_ref, inner_ref, act_ref, ecum_ref,
    q_ref, k_ref, v_ref, decay_ref, sq, sk, sv, sems,
):
    pairs = ((decay_hbm, decay_ref), (k_hbm, k_ref), (v_hbm, v_ref), (q_hbm, q_ref))
    copies = [pltpu.make_async_copy(a, b, sems.at[i]) for i, (a, b) in enumerate(pairs)]
    for copy in copies:
        copy.start()
    copies[0].wait()
    lane = lax.broadcasted_iota(jnp.int32, (HEADS, TOK), 1)
    cum = decay_ref[...]
    step = 1
    while step < TOK:
        cum = cum + jnp.where(lane >= step, pltpu.roll(cum, step, 1), 0.0)
        step *= 2
    cum_col = jnp.transpose(jnp.concatenate([cum] * (TOK // HEADS), axis=0))
    ecum_ref[...] = jnp.exp(cum_col)
    causal = lax.broadcasted_iota(jnp.int32, (TOK, TOK), 0) >= lax.broadcasted_iota(
        jnp.int32, (TOK, TOK), 1
    )
    copies[1].wait()
    sk[...] = silu(k_ref)
    copies[2].wait()
    sv[...] = silu(v_ref)
    copies[3].wait()
    sq[...] = silu(q_ref)
    for h in range(HEADS):
        mine = pl.ds(h, TOK, stride=HEADS)
        aq = sq[mine, :].astype(BF16)
        ak = sk[mine, :].astype(BF16)
        av = sv[mine, :].astype(BF16)
        act_ref[h] = aq
        row = cum[h : h + 1, :]
        col = cum_col[:, h : h + 1]
        last = row[:, TOK - 1 : TOK]
        scores = lax.dot_general(aq, ak, (((1,), (1,)), ((), ())), preferred_element_type=F32)
        weights = (scores * jnp.exp(jnp.where(causal, col - row, NEG))).astype(BF16)
        inner_ref[h] = jnp.dot(weights, av, preferred_element_type=F32)
        scaled = (ak.astype(F32) * jnp.exp(last - col)).astype(BF16)
        state = lax.dot_general(scaled, av, (((0,), (0,)), ((), ())), preferred_element_type=F32)
        extra = scalar_rows(jnp.broadcast_to(last, (1, 128)))
        for half in range(2):
            pay_ref[2 * h + half, 0:SLICE, :] = state[half * SLICE : (half + 1) * SLICE].astype(BF16)
            pay_ref[2 * h + half, SLICE:STATE_ROWS, :] = extra


def keep_kernel(pay_in, inner_ref, act_ref, ecum_ref, pay_out):
    pass


def row_kernel(got_ref, q_ref, pay_ref):
    run = jnp.zeros((SLICE, 128), F32)
    total = jnp.zeros((1, 128), F32)
    for z in range(Z):
        decay = scalar_back(got_ref[z, SLICE:STATE_ROWS, :])
        run = run * jnp.exp(decay) + got_ref[z, 0:SLICE, :].astype(F32)
        total = total + decay
    extra = scalar_rows(total)
    for y in range(Y):
        pay_ref[y, 0:SLICE, :] = run.astype(BF16)
        pay_ref[y, SLICE:STATE_ROWS, :] = extra
        pay_ref[y, STATE_ROWS:, :] = q_ref[...]


def carry_kernel(pos_ref, rows_ref, got_ref, out_ref):
    mine = pos_ref[0]
    run = jnp.zeros((SLICE, 128), F32)
    for y in range(Y - 1):
        decay = scalar_back(rows_ref[y, SLICE:STATE_ROWS, :])
        new = run * jnp.exp(decay) + rows_ref[y, 0:SLICE, :].astype(F32)
        run = jnp.where(y < mine, new, run)
    for z in range(Z):
        out_ref[z] = run.astype(BF16)
        decay = scalar_back(got_ref[z, SLICE:STATE_ROWS, :])
        run = run * jnp.exp(decay) + got_ref[z, 0:SLICE, :].astype(F32)


def mix_kernel(act_ref, inner_ref, ecum_ref, prior_ref, mixed_ref, square_ref):
    squares = jnp.zeros((TOK, HD), F32)
    for h in range(HEADS):
        outer = jnp.dot(act_ref[h], prior_ref[h * HD : (h + 1) * HD, :], preferred_element_type=F32)
        mixed = inner_ref[h] + outer * ecum_ref[:, h : h + 1]
        squares = squares + mixed * mixed
        mixed_ref[pl.ds(h, TOK, stride=HEADS), :] = mixed
    square_ref[...] = jnp.sum(jnp.transpose(squares), axis=0, keepdims=True)


QT = 512
CHUNK = 256
KEYS = Z * TOK


def attend_kernel(pos_ref, q_ref, kv_hbm, out_ref, keys, vaug, s_even, s_odd, stats, sems):
    my_y, my_z = pos_ref[0], pos_ref[1]
    get_keys = pltpu.make_async_copy(kv_hbm.at[:, 0:TOK, :], keys, sems.at[0])
    get_values = pltpu.make_async_copy(kv_hbm.at[:, TOK : 2 * TOK, :], vaug.at[:, :, 0:HD], sems.at[1])
    get_keys.start()
    get_values.start()
    vaug[:, :, HD:] = jnp.ones((Z, TOK, HD), BF16)
    get_keys.wait()
    get_values.wait()
    held = (s_even, s_odd)
    tiles, chunks, blocks = ROWS // QT, KEYS // CHUNK, CHUNK // TOK

    def score(y, i, j, top, masked):
        q = q_ref[y, STATE_ROWS + i * QT : STATE_ROWS + (i + 1) * QT, :]
        part = keys[j * blocks : (j + 1) * blocks].reshape(CHUNK, HD)
        s = lax.dot_general(q, part, (((1,), (1,)), ((), ())), preferred_element_type=F32)
        if masked:
            row = lax.broadcasted_iota(jnp.int32, (QT, CHUNK), 0)
            key = lax.broadcasted_iota(jnp.int32, (QT, CHUNK), 1)
            pos = my_z * TOK - j * CHUNK + (row + i * QT) // HEADS
            s = jnp.where(pos >= key, s, NEG)
        held[i % 2][:, j * CHUNK : (j + 1) * CHUNK] = s
        for lanes in range(blocks):
            new = s[:, lanes * 128 : (lanes + 1) * 128]
            top = new if top is None else jnp.maximum(top, new)
        return top

    def unit(y, masked):
        top = None
        for j in range(chunks):
            top = score(y, 0, j, top, masked)
        for i in range(tiles):
            shift = jnp.max(top, axis=1, keepdims=True) * SCALE2
            top = acc = None
            for j in range(chunks):
                if i + 1 < tiles:
                    top = score(y, i + 1, j, top, masked)
                s = held[i % 2][:, j * CHUNK : (j + 1) * CHUNK]
                p = jnp.exp2(s * SCALE2 - shift).astype(BF16)
                part = vaug[j * blocks : (j + 1) * blocks].reshape(CHUNK, 2 * HD)
                new = jnp.dot(p, part, preferred_element_type=F32)
                acc = new if acc is None else acc + new
            total = acc[:, HD:]
            out_ref[y, STAT_ROWS + i * QT : STAT_ROWS + (i + 1) * QT, :] = (acc[:, :HD] / total).astype(BF16)
            lse = shift + jnp.log(total) * LOG2E
            for b in range(QT // 128):
                at = i * (QT // 128) + b
                stats[at : at + 1, :] = jnp.transpose(lse[b * 128 : (b + 1) * 128])[0:1]
        high, mid, low = split3(stats[...])
        zero = jnp.zeros((HEADS, 128), BF16)
        out_ref[y, 0:16, :] = jnp.concatenate([high, mid], axis=0)
        out_ref[y, 16:32, :] = jnp.concatenate([low, zero], axis=0)

    def skip(y, carry):
        out_ref[y, 0:16, :] = jnp.concatenate([jnp.full((8, 128), NEG, BF16), jnp.zeros((8, 128), BF16)], axis=0)
        out_ref[y, 16:, :] = jnp.zeros((ROWS + 16, HD), BF16)
        return carry

    def other(y, carry):
        unit(y, False)
        return carry

    lax.fori_loop(0, my_y, skip, 0)
    unit(my_y, True)
    lax.fori_loop(my_y + 1, Y, other, 0)


def merge_kernel(got_ref, out_ref):
    lse = []
    for y in range(Y):
        first = got_ref[y, 0:16, :].astype(F32)
        second = got_ref[y, 16:32, :].astype(F32)
        lse.append(first[0:8] + first[8:16] + second[0:8])
    top = jnp.maximum(jnp.maximum(lse[0], lse[1]), jnp.maximum(lse[2], lse[3]))
    w = [jnp.exp2(x - top) for x in lse]
    total = w[0] + w[1] + w[2] + w[3]
    w = [x / total for x in w]
    for b in range(ROWS // 128):
        rows = slice(STAT_ROWS + b * 128, STAT_ROWS + (b + 1) * 128)
        acc = jnp.zeros((128, HD), F32)
        for y in range(Y):
            col = jnp.transpose(jnp.broadcast_to(w[y][b : b + 1, :], (128, 128)))
            acc = acc + col * got_ref[y, rows, :].astype(F32)
        out_ref[b * 128 : (b + 1) * 128, :] = acc.astype(BF16)


def shape(*dims, kind=BF16):
    return jax.ShapeDtypeStruct(dims, kind)


VM = pl.BlockSpec(memory_space=pltpu.VMEM)
SM = pl.BlockSpec(memory_space=pltpu.SMEM)
HB = pl.BlockSpec(memory_space=pltpu.HBM)
ANY = pl.BlockSpec(memory_space=pl.ANY)


def params(mib=16):
    return pltpu.CompilerParams(vmem_limit_bytes=mib << 20)


def cost(flops, nbytes, exps=0):
    return pl.CostEstimate(flops=flops, bytes_accessed=nbytes, transcendentals=exps)


def local(lin_query, lin_key, lin_value, log_decay, norm_gain, attn_query, attn_key, attn_value):
    index = lax.axis_index("ctx")
    pos = jnp.stack([lax.shift_right_logical(index, 4), index & (Z - 1)]).astype(jnp.int32)

    flat = lambda x: x.reshape(ROWS, HD)
    kv = [attn_key.reshape(TOK, HD), attn_value.reshape(TOK, HD), jnp.zeros((SPARE, HD), BF16)]
    kv = jnp.concatenate(kv, axis=0)
    kv = lax.all_gather(kv, "ctx", axis_index_groups=PAIR_GROUPS)
    kv, pos, lin_query, lin_key, lin_value = lax.optimization_barrier(
        (kv, pos, lin_query, lin_key, lin_value)
    )
    kv_row = lax.all_gather(kv, "ctx", axis_index_groups=SPREAD_GROUPS).reshape(Z, KV_ROWS, HD)
    pay, inner, act, ecum = pl.pallas_call(
        local_kernel,
        out_shape=(
            shape(Z, STATE_ROWS, 128),
            shape(HEADS, TOK, HD, kind=F32),
            shape(HEADS, TOK, HD),
            shape(TOK, 128, kind=F32),
        ),
        in_specs=[ANY] * 4,
        out_specs=(VM,) * 4,
        scratch_shapes=[pltpu.VMEM((ROWS, HD), BF16)] * 3
        + [pltpu.VMEM((HEADS, TOK), F32)]
        + [pltpu.VMEM((ROWS, HD), F32)] * 3
        + [pltpu.SemaphoreType.DMA((4,))],
        compiler_params=params(62),
        cost_estimate=cost(1, 1),
        name="local_part",
    )(flat(lin_query), flat(lin_key), flat(lin_value), log_decay)
    pay = pl.pallas_call(
        keep_kernel,
        out_shape=shape(Z, STATE_ROWS, 128),
        in_specs=[ANY] * 4,
        out_specs=ANY,
        input_output_aliases={0: 0},
        compiler_params=params(62),
        cost_estimate=cost(1, 1),
        name="keep",
    )(pay, inner, act, ecum)
    got = lax.all_to_all(pay, "ctx", 0, 0, axis_index_groups=Z_GROUPS)
    got, query = lax.optimization_barrier((got, flat(attn_query)))

    pay = pl.pallas_call(
        row_kernel,
        out_shape=shape(Y, STATE_ROWS + ROWS, 128),
        in_specs=[VM, VM],
        out_specs=VM,
        compiler_params=params(),
        cost_estimate=cost(1, 1),
        name="row_scan",
    )(got, query)
    queries = lax.all_to_all(pay, "ctx", 0, 0, axis_index_groups=Y_GROUPS)

    pay = pl.pallas_call(
        carry_kernel,
        out_shape=shape(Z, SLICE, 128),
        grid=(1,),
        in_specs=[
            SM,
            pl.BlockSpec((Y, STATE_ROWS, 128), lambda i: (0, 0, 0)),
            pl.BlockSpec((Z, STATE_ROWS, 128), lambda i: (0, 0, 0)),
        ],
        out_specs=pl.BlockSpec((Z, SLICE, 128), lambda i: (0, 0, 0)),
        compiler_params=params(),
        cost_estimate=cost(1, 1),
        name="carry_in",
    )(pos, queries, got)
    pay, queries = lax.optimization_barrier((pay, queries))
    prior = lax.all_to_all(pay, "ctx", 0, 0, axis_index_groups=Z_GROUPS)

    pay = pl.pallas_call(
        attend_kernel,
        out_shape=shape(Y, STAT_ROWS + ROWS, HD),
        in_specs=[SM, VM, HB],
        out_specs=VM,
        scratch_shapes=[
            pltpu.VMEM((Z, TOK, HD), BF16),
            pltpu.VMEM((Z, TOK, 2 * HD), BF16),
            pltpu.VMEM((QT, KEYS), F32),
            pltpu.VMEM((QT, KEYS), F32),
            pltpu.VMEM((HEADS, 128), F32),
            pltpu.SemaphoreType.DMA((2,)),
        ],
        compiler_params=params(62),
        cost_estimate=cost(3 * 2 * 4 * ROWS * KEYS * HD, 4 << 20, 4 * ROWS * KEYS),
        name="attend",
    )(pos, queries, kv_row)
    pay, prior = lax.optimization_barrier((pay, prior))
    got = lax.all_to_all(pay, "ctx", 0, 0, axis_index_groups=Y_GROUPS)

    mixed, squares = pl.pallas_call(
        mix_kernel,
        out_shape=(shape(ROWS, HD, kind=F32), shape(1, TOK, kind=F32)),
        in_specs=[VM] * 4,
        out_specs=(VM,) * 2,
        compiler_params=params(),
        cost_estimate=cost(2 * 8 * 128**3, 2 << 20),
        name="mix",
    )(act, inner, ecum, prior.reshape(ROWS, HD))

    total = lax.psum(squares, "head")
    inverse = lax.rsqrt(total[0] / (QUERY_HEADS * HD) + 1e-06)
    lin_out = mixed.reshape(TOK, HEADS, HD) * inverse[:, None, None] * norm_gain[None]
    lin_out = lin_out.astype(BF16)

    attn_out = pl.pallas_call(
        merge_kernel,
        out_shape=shape(ROWS, HD),
        in_specs=[VM],
        out_specs=VM,
        compiler_params=params(),
        cost_estimate=cost(1 << 20, 2 << 20),
        name="merge",
    )(got)
    return lin_out, attn_out.reshape(TOK, HEADS, HD)


def solution(mesh):
    act = P("ctx", "head", None)
    return jax.shard_map(
        local,
        mesh=mesh,
        in_specs=(act, act, act, P("head", "ctx"), P("head", None), act, act, act),
        out_specs=(act, act),
        check_vma=False,
    )
```

```python
import jax
import jax.numpy as jnp
from jax import lax
from jax.experimental import pallas as pl
from jax.experimental.pallas import tpu as pltpu
from jax.sharding import PartitionSpec as P

QUERY_HEADS = 64
HD = 128
TOK = 128
HEADS = 8
ROWS = TOK * HEADS
Y, Z = 4, 16
SLICE = ROWS // Z
STATE_ROWS = SLICE + 8
STAT_ROWS = 32
SPARE = 88
KV_ROWS = 2 * TOK + SPARE
LOG2E = 1.4426950408889634
SCALE2 = LOG2E * HD ** (-0.5)
NEG = -1e30
F32, BF16 = jnp.float32, jnp.bfloat16
Z_GROUPS = [[y * Z + z for z in range(Z)] for y in range(Y)]
PAIR_GROUPS = [[y * Z + 2 * p, y * Z + 2 * p + 1] for y in range(Y) for p in range(Z // 2)]
SPREAD_GROUPS = [[y * Z + 2 * p + odd for p in range(Z // 2)] for y in range(Y) for odd in range(2)]
Y_GROUPS = [[y * Z + z for y in range(Y)] for z in range(Z)]


def split3(x):
    high = x.astype(BF16)
    rest = x - high.astype(F32)
    mid = rest.astype(BF16)
    low = (rest - mid.astype(F32)).astype(BF16)
    return high, mid, low


def scalar_rows(x):
    high, mid, low = (part.astype(F32) for part in split3(x))
    row = lax.broadcasted_iota(jnp.int32, (8, 128), 0)
    out = jnp.where(row == 0, high, jnp.where(row == 1, mid, jnp.where(row == 2, low, 0.0)))
    return out.astype(BF16)


def scalar_back(rows):
    rows = rows.astype(F32)
    return rows[0:1] + rows[1:2] + rows[2:3]


def silu(ref):
    x = ref[...].astype(F32)
    return x / (1.0 + jnp.exp(-x))


def local_kernel(
    q_hbm, k_hbm, v_hbm, decay_hbm, pay_ref, inner_ref, act_ref, ecum_ref,
    q_ref, k_ref, v_ref, decay_ref, sq, sk, sv, sems,
):
    pairs = ((decay_hbm, decay_ref), (k_hbm, k_ref), (v_hbm, v_ref), (q_hbm, q_ref))
    copies = [pltpu.make_async_copy(a, b, sems.at[i]) for i, (a, b) in enumerate(pairs)]
    for copy in copies:
        copy.start()
    copies[0].wait()
    lane = lax.broadcasted_iota(jnp.int32, (HEADS, TOK), 1)
    cum = decay_ref[...]
    step = 1
    while step < TOK:
        cum = cum + jnp.where(lane >= step, pltpu.roll(cum, step, 1), 0.0)
        step *= 2
    cum_col = jnp.transpose(jnp.concatenate([cum] * (TOK // HEADS), axis=0))
    ecum_ref[...] = jnp.exp(cum_col)
    causal = lax.broadcasted_iota(jnp.int32, (TOK, TOK), 0) >= lax.broadcasted_iota(
        jnp.int32, (TOK, TOK), 1
    )
    copies[1].wait()
    sk[...] = silu(k_ref)
    copies[2].wait()
    sv[...] = silu(v_ref)
    copies[3].wait()
    sq[...] = silu(q_ref)
    for h in range(HEADS):
        mine = pl.ds(h, TOK, stride=HEADS)
        aq = sq[mine, :].astype(BF16)
        ak = sk[mine, :].astype(BF16)
        av = sv[mine, :].astype(BF16)
        act_ref[h] = aq
        row = cum[h : h + 1, :]
        col = cum_col[:, h : h + 1]
        last = row[:, TOK - 1 : TOK]
        scores = lax.dot_general(aq, ak, (((1,), (1,)), ((), ())), preferred_element_type=F32)
        weights = (scores * jnp.exp(jnp.where(causal, col - row, NEG))).astype(BF16)
        inner_ref[h] = jnp.dot(weights, av, preferred_element_type=F32)
        scaled = (ak.astype(F32) * jnp.exp(last - col)).astype(BF16)
        state = lax.dot_general(scaled, av, (((0,), (0,)), ((), ())), preferred_element_type=F32)
        extra = scalar_rows(jnp.broadcast_to(last, (1, 128)))
        for half in range(2):
            pay_ref[2 * h + half, 0:SLICE, :] = state[half * SLICE : (half + 1) * SLICE].astype(BF16)
            pay_ref[2 * h + half, SLICE:STATE_ROWS, :] = extra


def keep_kernel(pay_in, inner_ref, act_ref, ecum_ref, pay_out):
    pass


def row_kernel(got_ref, q_ref, pay_ref):
    run = jnp.zeros((SLICE, 128), F32)
    total = jnp.zeros((1, 128), F32)
    for z in range(Z):
        decay = scalar_back(got_ref[z, SLICE:STATE_ROWS, :])
        run = run * jnp.exp(decay) + got_ref[z, 0:SLICE, :].astype(F32)
        total = total + decay
    extra = scalar_rows(total)
    for y in range(Y):
        pay_ref[y, 0:SLICE, :] = run.astype(BF16)
        pay_ref[y, SLICE:STATE_ROWS, :] = extra
        pay_ref[y, STATE_ROWS:, :] = q_ref[...]


def carry_kernel(pos_ref, rows_ref, got_ref, out_ref):
    mine = pos_ref[0]
    run = jnp.zeros((SLICE, 128), F32)
    for y in range(Y - 1):
        decay = scalar_back(rows_ref[y, SLICE:STATE_ROWS, :])
        new = run * jnp.exp(decay) + rows_ref[y, 0:SLICE, :].astype(F32)
        run = jnp.where(y < mine, new, run)
    for z in range(Z):
        out_ref[z] = run.astype(BF16)
        decay = scalar_back(got_ref[z, SLICE:STATE_ROWS, :])
        run = run * jnp.exp(decay) + got_ref[z, 0:SLICE, :].astype(F32)


def mix_kernel(act_ref, inner_ref, ecum_ref, prior_ref, mixed_ref, square_ref):
    squares = jnp.zeros((TOK, HD), F32)
    for h in range(HEADS):
        outer = jnp.dot(act_ref[h], prior_ref[h * HD : (h + 1) * HD, :], preferred_element_type=F32)
        mixed = inner_ref[h] + outer * ecum_ref[:, h : h + 1]
        squares = squares + mixed * mixed
        mixed_ref[pl.ds(h, TOK, stride=HEADS), :] = mixed
    square_ref[...] = jnp.sum(jnp.transpose(squares), axis=0, keepdims=True)


QT = 512
CHUNK = 256
KEYS = Z * TOK


def attend_kernel(pos_ref, q_ref, kv_hbm, out_ref, keys, vaug, s_even, s_odd, stats, sems):
    my_y, my_z = pos_ref[0], pos_ref[1]
    get_keys = pltpu.make_async_copy(kv_hbm.at[:, 0:TOK, :], keys, sems.at[0])
    get_values = pltpu.make_async_copy(kv_hbm.at[:, TOK : 2 * TOK, :], vaug.at[:, :, 0:HD], sems.at[1])
    get_keys.start()
    get_values.start()
    vaug[:, :, HD:] = jnp.ones((Z, TOK, HD), BF16)
    get_keys.wait()
    get_values.wait()
    held = (s_even, s_odd)
    tiles, chunks, blocks = ROWS // QT, KEYS // CHUNK, CHUNK // TOK

    def score(y, i, j, top, masked):
        q = q_ref[y, STATE_ROWS + i * QT : STATE_ROWS + (i + 1) * QT, :]
        part = keys[j * blocks : (j + 1) * blocks].reshape(CHUNK, HD)
        s = lax.dot_general(q, part, (((1,), (1,)), ((), ())), preferred_element_type=F32)
        if masked:
            row = lax.broadcasted_iota(jnp.int32, (QT, CHUNK), 0)
            key = lax.broadcasted_iota(jnp.int32, (QT, CHUNK), 1)
            pos = my_z * TOK - j * CHUNK + (row + i * QT) // HEADS
            s = jnp.where(pos >= key, s, NEG)
        held[i % 2][:, j * CHUNK : (j + 1) * CHUNK] = s
        for lanes in range(blocks):
            new = s[:, lanes * 128 : (lanes + 1) * 128]
            top = new if top is None else jnp.maximum(top, new)
        return top

    def unit(y, masked):
        top = None
        for j in range(chunks):
            top = score(y, 0, j, top, masked)
        for i in range(tiles):
            shift = jnp.max(top, axis=1, keepdims=True) * SCALE2
            top = acc = None
            for j in range(chunks):
                if i + 1 < tiles:
                    top = score(y, i + 1, j, top, masked)
                s = held[i % 2][:, j * CHUNK : (j + 1) * CHUNK]
                p = jnp.exp2(s * SCALE2 - shift).astype(BF16)
                part = vaug[j * blocks : (j + 1) * blocks].reshape(CHUNK, 2 * HD)
                new = jnp.dot(p, part, preferred_element_type=F32)
                acc = new if acc is None else acc + new
            total = acc[:, HD:]
            out_ref[y, STAT_ROWS + i * QT : STAT_ROWS + (i + 1) * QT, :] = (acc[:, :HD] / total).astype(BF16)
            lse = shift + jnp.log(total) * LOG2E
            for b in range(QT // 128):
                at = i * (QT // 128) + b
                stats[at : at + 1, :] = jnp.transpose(lse[b * 128 : (b + 1) * 128])[0:1]
        high, mid, low = split3(stats[...])
        zero = jnp.zeros((HEADS, 128), BF16)
        out_ref[y, 0:16, :] = jnp.concatenate([high, mid], axis=0)
        out_ref[y, 16:32, :] = jnp.concatenate([low, zero], axis=0)

    def skip(y, carry):
        out_ref[y, 0:16, :] = jnp.concatenate([jnp.full((8, 128), NEG, BF16), jnp.zeros((8, 128), BF16)], axis=0)
        out_ref[y, 16:, :] = jnp.zeros((ROWS + 16, HD), BF16)
        return carry

    def other(y, carry):
        unit(y, False)
        return carry

    lax.fori_loop(0, my_y, skip, 0)
    unit(my_y, True)
    lax.fori_loop(my_y + 1, Y, other, 0)


def merge_kernel(got_ref, out_ref):
    lse = []
    for y in range(Y):
        first = got_ref[y, 0:16, :].astype(F32)
        second = got_ref[y, 16:32, :].astype(F32)
        lse.append(first[0:8] + first[8:16] + second[0:8])
    top = jnp.maximum(jnp.maximum(lse[0], lse[1]), jnp.maximum(lse[2], lse[3]))
    w = [jnp.exp2(x - top) for x in lse]
    total = w[0] + w[1] + w[2] + w[3]
    w = [x / total for x in w]
    for b in range(ROWS // 128):
        rows = slice(STAT_ROWS + b * 128, STAT_ROWS + (b + 1) * 128)
        acc = jnp.zeros((128, HD), F32)
        for y in range(Y):
            col = jnp.transpose(jnp.broadcast_to(w[y][b : b + 1, :], (128, 128)))
            acc = acc + col * got_ref[y, rows, :].astype(F32)
        out_ref[b * 128 : (b + 1) * 128, :] = acc.astype(BF16)


def shape(*dims, kind=BF16):
    return jax.ShapeDtypeStruct(dims, kind)


VM = pl.BlockSpec(memory_space=pltpu.VMEM)
SM = pl.BlockSpec(memory_space=pltpu.SMEM)
HB = pl.BlockSpec(memory_space=pltpu.HBM)
ANY = pl.BlockSpec(memory_space=pl.ANY)


def params(mib=16):
    return pltpu.CompilerParams(vmem_limit_bytes=mib << 20)


def cost(flops, nbytes, exps=0):
    return pl.CostEstimate(flops=flops, bytes_accessed=nbytes, transcendentals=exps)


def local(lin_query, lin_key, lin_value, log_decay, norm_gain, attn_query, attn_key, attn_value):
    index = lax.axis_index("ctx")
    pos = jnp.stack([lax.shift_right_logical(index, 4), index & (Z - 1)]).astype(jnp.int32)

    flat = lambda x: x.reshape(ROWS, HD)
    kv = [attn_key.reshape(TOK, HD), attn_value.reshape(TOK, HD), jnp.zeros((SPARE, HD), BF16)]
    kv = jnp.concatenate(kv, axis=0)
    kv = lax.all_gather(kv, "ctx", axis_index_groups=PAIR_GROUPS)
    kv, pos, lin_query, lin_key, lin_value = lax.optimization_barrier(
        (kv, pos, lin_query, lin_key, lin_value)
    )
    kv_row = lax.all_gather(kv, "ctx", axis_index_groups=SPREAD_GROUPS).reshape(Z, KV_ROWS, HD)
    pay, inner, act, ecum = pl.pallas_call(
        local_kernel,
        out_shape=(
            shape(Z, STATE_ROWS, 128),
            shape(HEADS, TOK, HD, kind=F32),
            shape(HEADS, TOK, HD),
            shape(TOK, 128, kind=F32),
        ),
        in_specs=[ANY] * 4,
        out_specs=(VM,) * 4,
        scratch_shapes=[pltpu.VMEM((ROWS, HD), BF16)] * 3
        + [pltpu.VMEM((HEADS, TOK), F32)]
        + [pltpu.VMEM((ROWS, HD), F32)] * 3
        + [pltpu.SemaphoreType.DMA((4,))],
        compiler_params=params(62),
        cost_estimate=cost(1, 1),
        name="local_part",
    )(flat(lin_query), flat(lin_key), flat(lin_value), log_decay)
    pay = pl.pallas_call(
        keep_kernel,
        out_shape=shape(Z, STATE_ROWS, 128),
        in_specs=[ANY] * 4,
        out_specs=ANY,
        input_output_aliases={0: 0},
        compiler_params=params(62),
        cost_estimate=cost(1, 1),
        name="keep",
    )(pay, inner, act, ecum)
    got = lax.all_to_all(pay, "ctx", 0, 0, axis_index_groups=Z_GROUPS)
    got, query = lax.optimization_barrier((got, flat(attn_query)))

    pay = pl.pallas_call(
        row_kernel,
        out_shape=shape(Y, STATE_ROWS + ROWS, 128),
        in_specs=[VM, VM],
        out_specs=VM,
        compiler_params=params(),
        cost_estimate=cost(1, 1),
        name="row_scan",
    )(got, query)
    queries = lax.all_to_all(pay, "ctx", 0, 0, axis_index_groups=Y_GROUPS)

    pay = pl.pallas_call(
        carry_kernel,
        out_shape=shape(Z, SLICE, 128),
        in_specs=[SM, VM, VM],
        out_specs=VM,
        compiler_params=params(),
        cost_estimate=cost(1, 1),
        name="carry_in",
    )(pos, queries, got)
    pay, queries = lax.optimization_barrier((pay, queries))
    prior = lax.all_to_all(pay, "ctx", 0, 0, axis_index_groups=Z_GROUPS)

    pay = pl.pallas_call(
        attend_kernel,
        out_shape=shape(Y, STAT_ROWS + ROWS, HD),
        in_specs=[SM, VM, HB],
        out_specs=VM,
        scratch_shapes=[
            pltpu.VMEM((Z, TOK, HD), BF16),
            pltpu.VMEM((Z, TOK, 2 * HD), BF16),
            pltpu.VMEM((QT, KEYS), F32),
            pltpu.VMEM((QT, KEYS), F32),
            pltpu.VMEM((HEADS, 128), F32),
            pltpu.SemaphoreType.DMA((2,)),
        ],
        compiler_params=params(62),
        cost_estimate=cost(3 * 2 * 4 * ROWS * KEYS * HD, 4 << 20, 4 * ROWS * KEYS),
        name="attend",
    )(pos, queries, kv_row)
    pay, prior = lax.optimization_barrier((pay, prior))
    got = lax.all_to_all(pay, "ctx", 0, 0, axis_index_groups=Y_GROUPS)

    mixed, squares = pl.pallas_call(
        mix_kernel,
        out_shape=(shape(ROWS, HD, kind=F32), shape(1, TOK, kind=F32)),
        in_specs=[VM] * 4,
        out_specs=(VM,) * 2,
        compiler_params=params(),
        cost_estimate=cost(2 * 8 * 128**3, 2 << 20),
        name="mix",
    )(act, inner, ecum, prior.reshape(ROWS, HD))

    total = lax.psum(squares, "head")
    inverse = lax.rsqrt(total[0] / (QUERY_HEADS * HD) + 1e-06)
    lin_out = mixed.reshape(TOK, HEADS, HD) * inverse[:, None, None] * norm_gain[None]
    lin_out = lin_out.astype(BF16)

    attn_out = pl.pallas_call(
        merge_kernel,
        out_shape=shape(ROWS, HD),
        in_specs=[VM],
        out_specs=VM,
        compiler_params=params(),
        cost_estimate=cost(1 << 20, 2 << 20),
        name="merge",
    )(got)
    return lin_out, attn_out.reshape(TOK, HEADS, HD)


def solution(mesh):
    act = P("ctx", "head", None)
    return jax.shard_map(
        local,
        mesh=mesh,
        in_specs=(act, act, act, P("head", "ctx"), P("head", None), act, act, act),
        out_specs=(act, act),
        check_vma=False,
    )
```
